32 devices in a mesh: seq: 4 (over z), head: 8 (over y, x, core).
Axes of the slice: x: 2, y: 2, z: 4, core: 2. Of those that a mesh axis runs over, the one named last changes fastest.
Arguments:
- lengths: int32 [16], replicated, may hold values from 128 to 8192, as said below
- page_owner: int32 [384], replicated, may hold values from 0 to 16, as said below
- page_index: int32 [384], replicated, may hold values from 0 to 127, as said below
- page_dest: int32 [384], replicated, may hold values from 0 to 383, as said below
- src_cache: bfloat16 [384, 8, 64, 256], P(('seq', 'head')), may hold values from -8 to 8
- queries: bfloat16 [2, 16, 4096], replicated, may hold values from -8 to 8
- new_kv: bfloat16 [2, 16, 8, 256], replicated, may hold values from -6 to 6
- hidden_in: bfloat16 [2, 16, 4096], P(None, None, ('seq', 'head')), may hold values from -60 to 60
- out_weight: bfloat16 [4096, 4096], P(None, ('seq', 'head')), may hold values from -1.5 to 1.5
- norm_gain: bfloat16 [4096], P(('seq', 'head')), may hold values from 0.099609375 to 1.8984375
- router: bfloat16 [4096, 8], P(('seq', 'head')), may hold values from -0.09375 to 0.09375
- routes: int32 [2, 16, 2], replicated, may hold values from 0 to 7, all different within a row
- w_gate: bfloat16 [8, 4096, 8192], P('seq', None, 'head'), may hold values from -0.09375 to 0.09375
- w_up: bfloat16 [8, 4096, 8192], P('seq', None, 'head'), may hold values from -0.09375 to 0.09375
- w_down: bfloat16 [8, 8192, 4096], P('seq', 'head'), may hold values from -0.0625 to 0.0625
Outputs:
- page_pool: bfloat16 [8, 384, 64, 256], P('head', 'seq')
- mixed: bfloat16 [2, 16, 4096], P(None, None, ('seq', 'head'))
The draws below stay inside these ranges and needn't reach their ends.
Inputs may be any that keep to these rules, and one draw needn't show every extreme that they name: Each length is at least 128; one equals 8192; the requests' pages, lengths[r] / 64 rounded up for request r, fit into the 384 pages. `page_owner`: request r owns exactly lengths[r] / 64 rounded up source pages; the other pages carry 16. `page_index`: the pages of request r carry 0 to their count minus 1, each once; pages without request carry 0. `page_dest`: A permutation. Slot g belongs to destination group ((g % 384) // 96) + g // 384. Of the 12 pages that one device holds (pages i * 12 to (i + 1) * 12 - 1), at most 3 go to one group, and every draw has a device that sends exactly 3 to some group.
All inputs are finite; a program needn't handle non-finite values.
Results may differ from the reference program's by a relative error of at most 0.009.
Values may be sent and summed in bfloat16 or wider, within the bound.
No kernel may reach another device: no remote copies, remote signals or barrier semaphores. Data moves between devices by JAX's collectives and lax.ppermute only.
A program may use at most 128 MiB of HBM per device.

```python
import math
import jax
import jax.numpy as jnp
from jax import lax

D = 4096
HQ = 32
KVH = 8
HD = 128
EXPERTS = 8
TOPK = 2
FF = 8192
PAGE = 64
MAXLEN = 8192
REQS = 16
STEPS = 2
PG_DEV = 12
NPAGES = 384
SLOTS = 384
SLOTS_DEV = 96
N_SEQ = 4
N_HEAD = 8


def page_plan(base_key):
    folded = jax.random.fold_in(base_key, 9001)
    subkeys = jax.random.split(folded, 5)
    raw_lengths = jax.random.randint(subkeys[0], (REQS,), 1, MAXLEN + 1)
    spare_room = (NPAGES - 3 * REQS) * PAGE - MAXLEN
    factor = (jnp.sum(raw_lengths) + spare_room - 1) // spare_room
    lengths = jnp.minimum(2 * PAGE + raw_lengths // factor, MAXLEN)
    longest = jax.random.randint(subkeys[1], (), 0, REQS)
    request_ids = jnp.arange(REQS, dtype=jnp.int32)
    lengths = jnp.where(request_ids == longest, MAXLEN, lengths).astype(jnp.int32)
    counts = (lengths + PAGE - 1) // PAGE
    page_ends = jnp.cumsum(counts)
    starts = page_ends - counts
    logical = jnp.arange(NPAGES, dtype=jnp.int32)
    owners = jnp.sum((logical[:, None] >= page_ends[None, :]).astype(jnp.int32), axis=1)
    first_page = jnp.sum(jnp.where(owners[:, None] == request_ids[None, :], starts[None, :], 0), axis=1)
    positions = jnp.where(owners < REQS, logical - first_page, 0)
    placed = jax.random.permutation(subkeys[2], NPAGES)
    page_owner = owners[placed].astype(jnp.int32)
    page_index = positions[placed].astype(jnp.int32)
    replicas = N_HEAD // KVH
    groups = N_SEQ * replicas
    shifts = jax.random.permutation(subkeys[3], groups)
    device = logical // PG_DEV
    target = (logical % PG_DEV + shifts[device % groups]) % groups
    onehot = (target[:, None] == jnp.arange(groups, dtype=jnp.int32)[None, :]).astype(jnp.int32)
    ranking = jnp.sum((jnp.cumsum(onehot, axis=0) - onehot) * onehot, axis=1)
    spot_order = jax.random.permutation(subkeys[4], SLOTS_DEV)[ranking]
    page_dest = target % replicas * SLOTS + target // replicas * SLOTS_DEV + spot_order
    return (lengths, page_owner, page_index, page_dest.astype(jnp.int32))


def draw_lengths(key, part):
    return page_plan(key)[0]


def draw_page_owner(key, part):
    return page_plan(key)[1]


def draw_page_index(key, part):
    return page_plan(key)[2]


def draw_page_dest(key, part):
    return page_plan(key)[3]


def draw_src_cache(key, part):
    full_shape = (NPAGES, KVH, PAGE, 2 * HD)
    values = jnp.clip(jax.random.normal(key, full_shape, jnp.float32), -6.0, 6.0)
    return values.astype(jnp.bfloat16)


def draw_queries(key, part):
    full_shape = (STEPS, REQS, HQ * HD)
    values = jnp.clip(jax.random.normal(key, full_shape, jnp.float32), -6.0, 6.0)
    return values.astype(jnp.bfloat16)


def draw_hidden_in(key, part):
    full_shape = (STEPS, REQS, D)
    subkeys = jax.random.split(key, 3)
    scales = jnp.exp(jax.random.uniform(subkeys[0], (STEPS, REQS, 1), jnp.float32, 0.0, math.log(10.0)))
    values = jnp.clip(jax.random.normal(subkeys[2], full_shape, jnp.float32), -6.0, 6.0) * scales
    return values.astype(jnp.bfloat16)


def steps_of(key, dims, cuts, low, largest):
    def one(position, parts):
        draws = jax.random.uniform(jax.random.fold_in(jax.random.fold_in(key, 6), position), (parts,), jnp.float32, low / len(cuts), largest / len(cuts))
        return jnp.repeat(jnp.exp(draws), dims[position] // parts).reshape((-1,) + (1,) * (len(dims) - position - 1))

    loudness = one(*cuts[0])
    for cut in cuts[1:]:
        loudness = loudness * one(*cut)
    return loudness


def picks_of(stream_key, rows, number_of, top, lift):
    order = jax.random.permutation(jax.random.fold_in(stream_key, 1), number_of)
    favour = order
    for power in range(3):
        favour = favour * favour // number_of
    favour = favour * lift // number_of
    lots = jax.random.randint(jax.random.fold_in(stream_key, 2), (rows, number_of), 0, 4096) + favour
    sure = jax.random.permutation(jax.random.fold_in(stream_key, 3), rows)[jnp.arange(number_of) % rows]
    lots = jnp.where(jnp.arange(rows)[:, None] == sure[None, :], 1 << 14, lots)
    score = lots * number_of + jnp.arange(number_of)
    return lax.top_k(score.astype(jnp.int32), top)[1].astype(jnp.int32)


def bell_draw(key, shape, scale, most, cuts=(), kind=jnp.bfloat16):
    values = scale * jax.random.normal(key, shape, jnp.float32)
    if cuts:
        values = values * steps_of(key, shape, cuts, -0.22, 0.18)
    return jnp.clip(values, -most, most).astype(kind)


def setup_inputs(seed: int = 0) -> dict:
    keys = jax.random.split(jax.random.key(seed), 16)
    return {
        "lengths": draw_lengths(jax.random.fold_in(keys[15], 71), 0),
        "page_owner": draw_page_owner(jax.random.fold_in(keys[15], 71), 0),
        "page_index": draw_page_index(jax.random.fold_in(keys[15], 71), 0),
        "page_dest": draw_page_dest(jax.random.fold_in(keys[15], 71), 0),
        "src_cache": draw_src_cache(jax.random.fold_in(keys[15], 71), 0),
        "queries": draw_queries(jax.random.fold_in(keys[15], 71), 0),
        "new_kv": bell_draw(keys[6], (STEPS, REQS, KVH, 2 * HD), 1.0, 6.0),
        "hidden_in": draw_hidden_in(jax.random.fold_in(keys[15], 71), 0),
        "out_weight": bell_draw(keys[8], (HQ * HD, D), (HQ * HD // 256) ** -0.5, 1.5, ((1, 32),)),
        "norm_gain": jnp.clip(1.0 + 0.18 * jax.random.normal(keys[9], (D,), jnp.float32), 0.099609375, 1.8984375).astype(jnp.bfloat16),
        "router": bell_draw(keys[10], (D, EXPERTS), D ** -0.5, 0.09375, ((0, 32),)),
        "routes": picks_of(keys[11], STEPS * REQS, EXPERTS, TOPK, 2048).reshape((STEPS, REQS, TOPK)),
        "w_gate": bell_draw(keys[12], (EXPERTS, D, FF), D ** -0.5, 0.09375, ((0, 4), (2, 8))),
        "w_up": bell_draw(keys[13], (EXPERTS, D, FF), D ** -0.5, 0.09375, ((0, 4), (2, 8))),
        "w_down": bell_draw(keys[14], (EXPERTS, FF, D), FF ** -0.5, 0.0625, ((0, 4), (1, 8))),
    }


NEG_FILL = -1e+30
EPSILON = 1e-05
HIGHEST = lax.Precision.HIGHEST

def gate_mix(logits, picked):
    expert_ids = jnp.arange(logits.shape[1], dtype=jnp.int32)[None, :]
    first_hit = picked[:, 0:1] == expert_ids
    second_hit = picked[:, 1:2] == expert_ids
    first_logit = lax.optimization_barrier(jnp.sum(jnp.where(first_hit, logits, 0.0), axis=1))
    second_logit = lax.optimization_barrier(jnp.sum(jnp.where(second_hit, logits, 0.0), axis=1))
    leading = 1.0 / (1.0 + jnp.exp(second_logit - first_logit))
    trailing = 1.0 / (1.0 + jnp.exp(first_logit - second_logit))
    return jnp.where(first_hit, leading[:, None], 0.0) + jnp.where(second_hit, trailing[:, None], 0.0)

def attend(lengths, page_owner, page_index, src_cache, queries, new_kv):
    step_count = queries.shape[0]
    group_size = HQ // KVH
    grouped = queries.astype(jnp.float32).reshape(step_count, REQS, KVH, group_size, HD)
    score_scale = HD ** (-0.5)
    clipped = jnp.minimum(page_owner, REQS - 1).astype(jnp.int32)
    offsets = page_index[:, None] * PAGE + jnp.arange(PAGE, dtype=jnp.int32)[None, :]
    is_live = (page_owner < REQS)[:, None] & (offsets < jnp.take(lengths, clipped)[:, None])
    asked_rows = jnp.take(grouped, clipped, axis=1)
    key_float = src_cache[..., :HD].astype(jnp.float32)
    scores = jnp.einsum('spkgd,pktd->spkgt', asked_rows, key_float, precision=HIGHEST) * score_scale
    live_mask = is_live[None, :, None, None, :]
    scores = jnp.where(live_mask, scores, NEG_FILL)
    members = page_owner[:, None] == jnp.arange(REQS, dtype=jnp.int32)[None, :]
    page_top = lax.optimization_barrier(jnp.max(scores, axis=4))
    row_top = lax.optimization_barrier(jnp.max(jnp.where(members[None, :, :, None, None], page_top[:, :, None], NEG_FILL), axis=1))
    fresh_keys = new_kv[..., :HD].astype(jnp.float32)
    fresh_values = new_kv[..., HD:].astype(jnp.float32)
    fresh_scores = jnp.einsum('srkgd,urkd->srkgu', grouped, fresh_keys, precision=HIGHEST) * score_scale
    causal = jnp.arange(step_count)[:, None] >= jnp.arange(step_count)[None, :]
    causal_mask = causal[:, None, None, None, :]
    fresh_scores = jnp.where(causal_mask, fresh_scores, NEG_FILL)
    row_top = jnp.maximum(row_top, lax.optimization_barrier(jnp.max(fresh_scores, axis=4)))
    weights = jnp.where(live_mask, jnp.exp(scores - jnp.take(row_top, clipped, axis=1)[..., None]), 0.0)
    fresh_weights = jnp.where(causal_mask, jnp.exp(fresh_scores - row_top[..., None]), 0.0)
    member_mask = members.astype(jnp.float32)
    totals = jnp.einsum('pr,spkg->srkg', member_mask, lax.optimization_barrier(jnp.sum(weights, axis=4)), precision=HIGHEST)
    totals = totals + lax.optimization_barrier(jnp.sum(fresh_weights, axis=4))
    rounded = lax.optimization_barrier(weights.astype(jnp.bfloat16)).astype(jnp.float32)
    page_out = jnp.einsum('spkgt,pktd->spkgd', rounded, src_cache[..., HD:].astype(jnp.float32), precision=HIGHEST)
    weighted = jnp.einsum('pr,spkgd->srkgd', member_mask, page_out, precision=HIGHEST)
    fresh_rounded = lax.optimization_barrier(fresh_weights.astype(jnp.bfloat16)).astype(jnp.float32)
    weighted = weighted + jnp.einsum('srkgu,urkd->srkgd', fresh_rounded, fresh_values, precision=HIGHEST)
    return (weighted / totals[..., None]).reshape(step_count, REQS, HQ * HD).astype(jnp.bfloat16)

def reference(lengths, page_owner, page_index, page_dest, src_cache, queries, new_kv, hidden_in, out_weight, norm_gain, router, routes, w_gate, w_up, w_down):
    replicas = N_HEAD // KVH
    slot_count = NPAGES // replicas
    inverse = jnp.argsort(page_dest).astype(jnp.int32)
    ordered = jnp.take(src_cache, inverse, axis=0)
    page_pool = ordered.reshape(replicas, slot_count, KVH, PAGE, 2 * HD).transpose(2, 0, 1, 3, 4)
    page_pool = page_pool.reshape(KVH * replicas, slot_count, PAGE, 2 * HD)
    attended = attend(lengths, page_owner, page_index, src_cache, queries, new_kv)
    step_count = queries.shape[0]
    row_count = step_count * REQS
    attn_out = jnp.dot(attended.reshape(row_count, HQ * HD), out_weight, preferred_element_type=jnp.float32)
    middle = hidden_in.reshape(row_count, D).astype(jnp.float32) + attn_out
    inverse_rms = lax.rsqrt(lax.optimization_barrier(jnp.mean(middle * middle, axis=1, keepdims=True)) + EPSILON)
    normed = middle * inverse_rms * norm_gain.astype(jnp.float32)[None, :]
    logits = jnp.dot(normed, router.astype(jnp.float32), precision=HIGHEST)
    mixture = gate_mix(logits, routes.reshape(row_count, TOPK))
    features = normed.astype(jnp.bfloat16)

    def one_expert(running, expert):
        gate_act = jnp.dot(features, w_gate[expert], preferred_element_type=jnp.float32)
        upward = jnp.dot(features, w_up[expert], preferred_element_type=jnp.float32)
        inner_act = (jax.nn.silu(gate_act) * upward).astype(jnp.bfloat16)
        produced = jnp.dot(inner_act, w_down[expert], preferred_element_type=jnp.float32)
        expert_share = lax.optimization_barrier(jnp.sum(jnp.where(jnp.arange(EXPERTS, dtype=jnp.int32)[None, :] == expert, mixture, 0.0), axis=1))
        return (running + expert_share[:, None] * produced, None)
    moe_out, unused = lax.scan(one_expert, jnp.zeros((row_count, D), jnp.float32), jnp.arange(EXPERTS, dtype=jnp.int32))
    mixed = (middle + moe_out).astype(jnp.bfloat16).reshape(step_count, REQS, D)
    return (page_pool, mixed)
```

```python
import functools

import jax
import jax.numpy as jnp
from jax import lax
from jax.experimental import pallas as pl
from jax.experimental.pallas import tpu as pltpu
from jax.sharding import PartitionSpec as P

D = 4096
HQ = 32
KVH = 8
HD = 128
TOPK = 2
PAGE = 64
REQS = 16
LANES = 128
STAT = 16

NEG_FILL = -1e30
EPSILON = 1e-05
HIGHEST = lax.Precision.HIGHEST
VMEM_SPEC = pl.BlockSpec(memory_space=pltpu.VMEM)


def shift_perm(count, shift):
    return [(i, (i + shift) % count) for i in range(count)]


def pieces(value):
    hi = value.astype(jnp.bfloat16).astype(jnp.float32)
    rest = value - hi
    mid = rest.astype(jnp.bfloat16).astype(jnp.float32)
    return hi, mid, rest - mid


def eye_mask(rows):
    return lax.broadcasted_iota(jnp.int32, (rows, LANES), 0) == lax.broadcasted_iota(
        jnp.int32, (rows, LANES), 1
    )


def to_lanes(column):
    rows = column.shape[0]
    return jnp.sum(
        jnp.where(eye_mask(rows), jnp.broadcast_to(column, (rows, LANES)), 0.0),
        axis=0,
        keepdims=True,
    )


def to_column(row, rows):
    return jnp.sum(
        jnp.where(eye_mask(rows), jnp.broadcast_to(row, (rows, LANES)), 0.0), axis=1, keepdims=True
    )


def stat_block(row):
    hi, mid, low = pieces(row)
    index = lax.broadcasted_iota(jnp.int32, (STAT, LANES), 0)
    block = jnp.where(index == 0, hi, jnp.where(index == 1, mid, jnp.where(index == 2, low, 0.0)))
    return block.astype(jnp.bfloat16)


def pack_kernel(picked_ref, page_ref, out_ref):
    out_ref[...] = jnp.swapaxes(page_ref[...], 0, 1)


def pack_pages(picked, src_cache):
    count = picked.shape[0]
    heads, page_len, width = src_cache.shape[1:]
    return pl.pallas_call(
        pack_kernel,
        out_shape=jax.ShapeDtypeStruct((heads, count, page_len, width), src_cache.dtype),
        grid_spec=pltpu.PrefetchScalarGridSpec(
            num_scalar_prefetch=1,
            grid=(count,),
            in_specs=[
                pl.BlockSpec((1, heads, page_len, width), lambda i, picked_ref: (picked_ref[i], 0, 0, 0))
            ],
            out_specs=pl.BlockSpec((heads, 1, page_len, width), lambda i, picked_ref: (0, i, 0, 0)),
        ),
        cost_estimate=pl.CostEstimate(
            flops=0, transcendentals=0, bytes_accessed=2 * count * heads * page_len * width * 2
        ),
    )(picked, src_cache)


def place_kernel(aliased, shift, seq_count, spots_ref, pages_ref, *rest):
    out_ref, sems = rest[-2], rest[-1]
    count = pages_ref.shape[0]
    me = lax.axis_index("seq")
    base = lax.rem(me - shift + seq_count, seq_count) * count

    def copy(i):
        spot = spots_ref[base + i]
        return spot >= 0, pltpu.make_async_copy(
            pages_ref.at[i], out_ref.at[jnp.maximum(spot, 0)], sems.at[i]
        )

    for i in range(count):
        there, move = copy(i)

        @pl.when(there)
        def _():
            move.start()

    for i in range(count):
        there, move = copy(i)

        @pl.when(there)
        def _():
            move.wait()


def place_pages(spots, pages, pool, slots_dev, shift, seq_count):
    count = pages.shape[0]
    aliased = pool is not None
    args = (spots, pages) + ((pool,) if aliased else ())
    return pl.pallas_call(
        functools.partial(place_kernel, aliased, shift, seq_count),
        out_shape=jax.ShapeDtypeStruct((slots_dev,) + pages.shape[1:], pages.dtype),
        in_specs=[pl.BlockSpec(memory_space=pltpu.SMEM), VMEM_SPEC]
        + ([pl.BlockSpec(memory_space=pl.ANY)] if aliased else []),
        out_specs=pl.BlockSpec(memory_space=pl.ANY),
        scratch_shapes=[pltpu.SemaphoreType.DMA((count,))],
        input_output_aliases={2: 0} if aliased else {},
    )(*args)


def attend_kernel(
    group,
    devices,
    where_ref,
    owner_ref,
    index_ref,
    length_ref,
    query_ref,
    fresh_ref,
    pages_ref,
    out_ref,
    top_ref,
    sum_ref,
    acc_ref,
):
    step = pl.program_id(0)
    requests, rows, head_dim = query_ref.shape
    heads, page_len = pages_ref.shape[1:3]
    per_head = rows // heads
    scale = head_dim ** (-0.5)
    source = where_ref[0]

    @pl.when(step == 0)
    def _():
        top_ref[...] = jnp.full_like(top_ref, NEG_FILL)
        sum_ref[...] = jnp.zeros_like(sum_ref)
        acc_ref[...] = jnp.zeros_like(acc_ref)

    def partial(request, keys, values, mask):
        scores = (
            lax.dot_general(
                query_ref[request], keys, (((1,), (1,)), ((), ())), preferred_element_type=jnp.float32
            )
            * scale
        )
        scores = jnp.where(mask, scores, NEG_FILL)
        top = jnp.max(scores, axis=1, keepdims=True)
        weights = jnp.where(mask, jnp.exp(scores - top), 0.0)
        total = jnp.sum(weights, axis=1, keepdims=True)
        out = jnp.dot(weights.astype(jnp.bfloat16), values, preferred_element_type=jnp.float32)
        return top, total, out

    def merge(request, part):
        top, total, out = part
        old = top_ref[request]
        top = jnp.broadcast_to(top, old.shape)
        new = jnp.maximum(old, top)
        keep = jnp.exp(old - new)
        gain = jnp.exp(top - new)
        top_ref[request] = new
        sum_ref[request] = sum_ref[request] * keep + gain * total
        acc_ref[request] = acc_ref[request] * keep + gain * out

    columns = heads * page_len
    row_head = lax.broadcasted_iota(jnp.int32, (rows, columns), 0) // per_head
    column = lax.broadcasted_iota(jnp.int32, (rows, columns), 1)
    same_head = row_head == column // page_len
    token = column % page_len
    parts = []
    for i in range(group):
        page = source * (group * pl.num_programs(0)) + step * group + i
        owner = owner_ref[page]
        request = jnp.minimum(owner, requests - 1)
        alive = jnp.where(
            owner < requests, length_ref[request] - index_ref[page] * page_len, 0
        )
        keys = pages_ref[i, :, :, :head_dim].reshape(columns, head_dim)
        values = pages_ref[i, :, :, head_dim:].reshape(columns, head_dim)
        parts.append((request, partial(request, keys, values, same_head & (token < alive))))
    for request, part in parts:
        merge(request, part)

    @pl.when(step == pl.num_programs(0) - 1)
    def _():
        head_count = out_ref.shape[0]
        block = rows // head_count
        fresh_rows = fresh_ref.shape[1]
        steps = fresh_rows // heads
        row = lax.broadcasted_iota(jnp.int32, (rows, fresh_rows), 0)
        col = lax.broadcasted_iota(jnp.int32, (rows, fresh_rows), 1)
        row_step = (row % block) // (block // steps)
        mask = (row // per_head == col % heads) & (col // heads <= row_step)
        for extra in range((requests + devices - 1) // devices):
            request = source + extra * devices

            @pl.when(request < requests)
            def _():
                keys = fresh_ref[request, :, :head_dim]
                values = fresh_ref[request, :, head_dim:]
                merge(request, partial(request, keys, values, mask))

        span = requests * block
        for dest in range(head_count):
            part = pl.ds(dest * block, block)
            total = sum_ref[:, part, :].reshape(span, LANES)
            top = top_ref[:, part, :].reshape(span, LANES)
            acc = acc_ref[:, part, :].reshape(span, LANES)
            some = total > 0.0
            safe = jnp.where(some, total, 1.0)
            out_ref[dest, :span, :] = (acc / safe).astype(jnp.bfloat16)
            joint = jnp.where(some, top + jnp.log(safe), NEG_FILL)
            row_vec = jnp.sum(jnp.where(eye_mask(span), joint, 0.0), axis=0, keepdims=True)
            out_ref[dest, span:, :] = stat_block(row_vec)


def partial_attention(source, owner, index, lengths, query, fresh, pages, head_count, devices):
    requests, rows, head_dim = query.shape
    page_count, heads, page_len, width = pages.shape
    group = max(g for g in (1, 2, 3, 4) if page_count % g == 0)
    span = requests * rows // head_count
    whole = lambda shape: pl.BlockSpec(shape, lambda i, *refs: (0,) * len(shape))
    return pl.pallas_call(
        functools.partial(attend_kernel, group, devices),
        out_shape=jax.ShapeDtypeStruct((head_count, span + STAT, LANES), jnp.bfloat16),
        grid_spec=pltpu.PrefetchScalarGridSpec(
            num_scalar_prefetch=4,
            grid=(page_count // group,),
            in_specs=[
                whole(query.shape),
                whole(fresh.shape),
                pl.BlockSpec((group, heads, page_len, width), lambda i, *refs: (i, 0, 0, 0)),
            ],
            out_specs=whole((head_count, span + STAT, LANES)),
            scratch_shapes=[pltpu.VMEM((requests, rows, LANES), jnp.float32)] * 3,
        ),
        cost_estimate=pl.CostEstimate(
            flops=4 * page_count * rows * heads * page_len * head_dim,
            transcendentals=page_count * rows * heads * page_len,
            bytes_accessed=2 * page_count * heads * page_len * width,
        ),
    )(source, owner, index, lengths, query, fresh, pages)


def mix_partials(blocks, span):
    rows = []
    for block in blocks:
        stats = block[span:, :].astype(jnp.float32)
        rows.append(stats[0:1] + stats[1:2] + stats[2:3])
    top = functools.reduce(jnp.maximum, rows)
    weights = [jnp.exp(row - top) for row in rows]
    total = sum(weights)
    out = 0.0
    for block, weight in zip(blocks, weights):
        out = out + to_column(weight / total, span) * block[:span, :].astype(jnp.float32)
    return out, top + jnp.log(total)


def gather_partials_kernel(parts_ref, out_ref):
    count, size, _ = parts_ref.shape
    span = size - STAT
    out, joint = mix_partials([parts_ref[i] for i in range(count)], span)
    out_ref[:span, :] = out.astype(jnp.bfloat16)
    out_ref[span:, :] = stat_block(joint)


def gather_partials(parts):
    return pl.pallas_call(
        gather_partials_kernel,
        out_shape=jax.ShapeDtypeStruct(parts.shape[1:], parts.dtype),
        in_specs=[VMEM_SPEC],
        out_specs=VMEM_SPEC,
    )(parts)


def finish_attention_kernel(steps, *refs):
    out_ref, flat_ref = refs[-2:]
    blocks = [ref[...] for ref in refs[:-2]]
    span = blocks[0].shape[0] - STAT
    out, _ = mix_partials(blocks, span)
    flat_ref[...] = out
    block = span // REQS
    per_step = block // steps
    for s in range(steps):
        for a in range(per_step):
            out_ref[s * REQS : (s + 1) * REQS, a * HD : (a + 1) * HD] = flat_ref[
                pl.ds(s * per_step + a, REQS, stride=block), :
            ].astype(jnp.bfloat16)


def finish_attention(blocks, steps):
    span = blocks[0].shape[0] - STAT
    per_step = span // REQS // steps
    return pl.pallas_call(
        functools.partial(finish_attention_kernel, steps),
        out_shape=jax.ShapeDtypeStruct((steps * REQS, per_step * HD), jnp.bfloat16),
        in_specs=[VMEM_SPEC] * len(blocks),
        out_specs=VMEM_SPEC,
        scratch_shapes=[pltpu.VMEM((span, LANES), jnp.float32)],
    )(*blocks)


def project_kernel(att_ref, weight_ref, hidden_ref, gain_ref, router_ref, middle_ref, out_ref):
    heads, rows, depth = att_ref.shape
    total = jnp.zeros(middle_ref.shape, jnp.float32)
    for h in range(heads):
        total = total + jnp.dot(
            att_ref[h], weight_ref[h * depth : (h + 1) * depth, :], preferred_element_type=jnp.float32
        )
    middle = hidden_ref[...].astype(jnp.float32) + total
    middle_ref[...] = middle
    scaled = middle * gain_ref[...].astype(jnp.float32)
    width = middle.shape[1]
    if width < LANES:
        out_ref[:rows, :] = jnp.zeros((rows, LANES), jnp.bfloat16)
    out_ref[:rows, :width] = scaled.astype(jnp.bfloat16)
    squares = jnp.sum(middle * middle, axis=1, keepdims=True)
    routed = jnp.dot(
        scaled,
        router_ref[...].astype(jnp.float32),
        precision=HIGHEST,
        preferred_element_type=jnp.float32,
    )
    lane = lax.broadcasted_iota(jnp.int32, (rows, LANES), 1)
    stats = jnp.where(lane == 8, squares, routed)
    out_ref[rows:, :] = spread_stats(stats)


def spread_stats(stats):
    hi, mid, low = pieces(stats)
    return (hi + pltpu.roll(mid, 16, 1) + pltpu.roll(low, 32, 1)).astype(jnp.bfloat16)


def joined_stats(block):
    wide = block.astype(jnp.float32)
    lane = lax.broadcasted_iota(jnp.int32, wide.shape, 1)
    total = wide + pltpu.roll(wide, LANES - 16, 1) + pltpu.roll(wide, LANES - 32, 1)
    return jnp.where(lane < 16, total, 0.0)


def project(att, weight, hidden, gain, router):
    rows, width = hidden.shape
    return pl.pallas_call(
        project_kernel,
        out_shape=(
            jax.ShapeDtypeStruct((rows, width), jnp.float32),
            jax.ShapeDtypeStruct((2 * rows, LANES), jnp.bfloat16),
        ),
        in_specs=[VMEM_SPEC] * 5,
        out_specs=(VMEM_SPEC, VMEM_SPEC),
    )(att, weight, hidden, gain, router)


def stack_kernel(*refs):
    out_ref = refs[-1]
    parts = refs[:-1]
    count = len(parts)
    rows = parts[0].shape[0] // 2
    me = lax.axis_index("seq")
    stats = 0.0
    for shift, ref in enumerate(parts):
        origin = lax.rem(me - shift + count, count)
        out_ref[origin] = ref[:rows, :]
        stats = stats + joined_stats(ref[rows:, :])
    out_ref[count] = spread_stats(stats)


def stack_parts(parts):
    rows = parts[0].shape[0] // 2
    return pl.pallas_call(
        stack_kernel,
        out_shape=jax.ShapeDtypeStruct((len(parts) + 1, rows, LANES), jnp.bfloat16),
        in_specs=[VMEM_SPEC] * len(parts),
        out_specs=VMEM_SPEC,
    )(*parts)


def features_kernel(local_experts, all_ref, routes_ref, feat_ref, aux_ref):
    heads, blocks, rows, _ = all_ref.shape
    seqs = blocks - 1
    width = feat_ref.shape[1] // (seqs * heads)
    for h in range(heads):
        for s in range(seqs):
            at = (s * heads + h) * width
            feat_ref[:, at : at + width] = all_ref[h, s, :, :width]
    stats = 0.0
    for h in range(heads):
        stats = stats + joined_stats(all_ref[h, seqs])
    lane = lax.broadcasted_iota(jnp.int32, (rows, LANES), 1)
    squares = jnp.sum(jnp.where(lane == 8, stats, 0.0), axis=1, keepdims=True)
    inverse = lax.rsqrt(squares / feat_ref.shape[1] + EPSILON)
    logits = stats * inverse
    first = routes_ref[:, 0:1] == lane
    second = routes_ref[:, 1:2] == lane
    first_logit = jnp.sum(jnp.where(first, logits, 0.0), axis=1, keepdims=True)
    second_logit = jnp.sum(jnp.where(second, logits, 0.0), axis=1, keepdims=True)
    leading = 1.0 / (1.0 + jnp.exp(second_logit - first_logit))
    trailing = 1.0 / (1.0 + jnp.exp(first_logit - second_logit))
    mixture = jnp.where(first, leading, 0.0) + jnp.where(second, trailing, 0.0)
    base = lax.axis_index("seq") * local_experts
    aux = jnp.where(lane == 0, inverse, 0.0)
    for e in range(local_experts):
        share = jnp.sum(jnp.where(lane == base + e, mixture, 0.0), axis=1, keepdims=True)
        aux = jnp.where(lane == 1 + e, share, aux)
    aux_ref[...] = aux


def features_of(everything, routes, local_experts, width):
    heads, blocks, rows, _ = everything.shape
    return pl.pallas_call(
        functools.partial(features_kernel, local_experts),
        out_shape=(
            jax.ShapeDtypeStruct((rows, heads * (blocks - 1) * width), jnp.bfloat16),
            jax.ShapeDtypeStruct((rows, LANES), jnp.float32),
        ),
        in_specs=[VMEM_SPEC] * 2,
        out_specs=(VMEM_SPEC, VMEM_SPEC),
    )(everything, routes)


def spread(block, axis):
    count = lax.axis_size(axis)
    return lax.all_to_all(
        jnp.broadcast_to(block[None], (count,) + block.shape), axis, 0, 0, tiled=True
    )


def body(
    lengths,
    page_owner,
    page_index,
    page_dest,
    src_cache,
    queries,
    new_kv,
    hidden_in,
    out_weight,
    norm_gain,
    router,
    routes,
    w_gate,
    w_up,
    w_down,
):
    seq_count = lax.axis_size("seq")
    head_count = lax.axis_size("head")
    device_count = seq_count * head_count
    seq_pos = lax.axis_index("seq")
    head_pos = lax.axis_index("head")
    pages_dev = src_cache.shape[0]
    page_total = page_dest.shape[0]
    replicas = head_count // KVH
    slot_count = page_total // replicas
    slots_dev = pages_dev * KVH
    capacity = (slots_dev + device_count - 1) // device_count
    step_count = queries.shape[0]
    row_count = step_count * REQS
    heads_dev = HQ // head_count
    source = seq_pos * head_count + head_pos

    part_index = page_dest // slot_count
    within = page_dest % slot_count
    target_seq = within // slots_dev
    position = within % slots_dev
    before = jnp.arange(pages_dev)[:, None] > jnp.arange(pages_dev)[None, :]
    local_part = lax.dynamic_slice_in_dim(part_index, source * pages_dev, pages_dev)
    local_seq = lax.dynamic_slice_in_dim(target_seq, source * pages_dev, pages_dev)
    bin_of = (local_seq + seq_count - seq_pos) % seq_count * replicas + local_part
    rank = jnp.sum(((bin_of[:, None] == bin_of[None, :]) & before).astype(jnp.int32), axis=1)
    wanted = jnp.arange(seq_count * replicas * capacity, dtype=jnp.int32)
    picked = jnp.sum(
        jnp.where(
            (bin_of * capacity + rank)[None, :] == wanted[:, None],
            jnp.arange(pages_dev, dtype=jnp.int32)[None, :],
            0,
        ),
        axis=1,
    )
    mine = ((target_seq == seq_pos) & (part_index == head_pos % replicas)).reshape(-1, pages_dev)
    mine_rank = jnp.sum((mine[:, None, :] & before[None]).astype(jnp.int32), axis=2)
    spots = jnp.sum(
        jnp.where(
            mine[:, None, :]
            & (mine_rank[:, None, :] == jnp.arange(capacity, dtype=jnp.int32)[None, :, None]),
            position.reshape(-1, pages_dev)[:, None, :] + 1,
            0,
        ),
        axis=2,
    )
    spots = spots.reshape(-1) - 1

    bin_size = replicas * capacity
    moved = []
    for shift in range(seq_count):
        packed = pack_pages(picked[shift * bin_size : (shift + 1) * bin_size], src_cache)
        packed = packed.reshape(head_count, capacity, PAGE, 2 * HD)
        if shift:
            packed = lax.ppermute(packed, "seq", shift_perm(seq_count, shift))
        moved.append(packed)

    query = (
        queries.reshape(step_count, REQS, head_count, heads_dev, HD)
        .transpose(1, 2, 0, 3, 4)
        .reshape(REQS, step_count * HQ, HD)
    )
    fresh = new_kv.transpose(1, 0, 2, 3).reshape(REQS, step_count * KVH, 2 * HD)
    parts = partial_attention(
        jnp.reshape(source, (1,)),
        page_owner,
        page_index,
        lengths,
        query,
        fresh,
        src_cache,
        head_count,
        device_count,
    )
    parts = lax.all_to_all(parts, "head", 0, 0, tiled=True)
    part = gather_partials(parts)
    blocks = [part] + [
        lax.ppermute(part, "seq", shift_perm(seq_count, shift)) for shift in range(1, seq_count)
    ]
    attended = finish_attention(blocks, step_count)
    attended = spread(attended, "head").reshape(head_count, row_count, heads_dev * HD)

    middle, payload = project(
        attended,
        out_weight,
        hidden_in.reshape(row_count, -1),
        norm_gain.reshape(1, -1),
        jnp.pad(router, ((0, 0), (0, LANES - router.shape[1]))),
    )
    payloads = [payload] + [
        lax.ppermute(payload, "seq", shift_perm(seq_count, shift)) for shift in range(1, seq_count)
    ]
    stacked = stack_parts(payloads)
    everything = spread(stacked, "head").reshape((head_count,) + stacked.shape)
    local_experts = w_gate.shape[0]
    features, aux = features_of(everything, routes.reshape(row_count, TOPK), local_experts, hidden_in.shape[2])
    inverse = aux[:, 0:1]
    gate_act = jnp.einsum("rd,edf->erf", features, w_gate, preferred_element_type=jnp.float32)
    upward = jnp.einsum("rd,edf->erf", features, w_up, preferred_element_type=jnp.float32)
    inner_act = (jax.nn.silu(gate_act * inverse) * (upward * inverse)).astype(jnp.bfloat16)
    produced = jnp.einsum("erf,efd->erd", inner_act, w_down, preferred_element_type=jnp.float32)
    local_mix = aux[:, 1 : 1 + local_experts]
    terms = jnp.sum(local_mix.T[:, :, None] * produced, axis=0).astype(jnp.bfloat16)
    terms = terms.reshape(row_count, seq_count, head_count, -1).transpose(2, 1, 0, 3)
    terms = lax.all_to_all(terms, "head", 0, 0, tiled=True)
    plane = jnp.sum(terms.astype(jnp.float32), axis=0)
    moe_out = lax.dynamic_index_in_dim(plane, seq_pos, 0, keepdims=False)
    plane = plane.astype(jnp.bfloat16)
    for shift in range(1, seq_count):
        share = lax.dynamic_index_in_dim(plane, (seq_pos + shift) % seq_count, 0, keepdims=False)
        moe_out = moe_out + lax.ppermute(share, "seq", shift_perm(seq_count, shift)).astype(
            jnp.float32
        )
    mixed = (middle + moe_out).astype(jnp.bfloat16).reshape(step_count, REQS, -1)

    pool = None
    for shift in range(seq_count):
        arrived = lax.all_to_all(moved[shift], "head", 0, 0, tiled=True)
        arrived = arrived.reshape(head_count * capacity, PAGE, 2 * HD)
        pool = place_pages(spots, arrived, pool, slots_dev, shift, seq_count)
    return (pool[None], mixed)


def solution(mesh):
    in_specs = (
        P(),
        P(),
        P(),
        P(),
        P(("seq", "head"), None, None, None),
        P(),
        P(),
        P(None, None, ("seq", "head")),
        P(None, ("seq", "head")),
        P(("seq", "head")),
        P(("seq", "head"), None),
        P(),
        P("seq", None, "head"),
        P("seq", None, "head"),
        P("seq", "head", None),
    )
    out_specs = (P("head", "seq", None, None), P(None, None, ("seq", "head")))
    return jax.shard_map(body, mesh=mesh, in_specs=in_specs, out_specs=out_specs, check_vma=False)
```
